256 devices in a mesh: row: 16 (over x_hi, y, core), col: 16 (over x_lo, z).
Axes of the slice: x: 4 (x_hi: 2, x_lo: 2; x = x_hi * 2 + x_lo), y: 4, z: 8, core: 2. Of those that a mesh axis runs over, the one named last changes fastest.
Arguments:
- points: bfloat16 [16, 131072], P(None, ('row', 'col')), may hold values from -6 to 6
- spread: bfloat16 [131072], P(('row', 'col')), may hold values from 2 to 12
- vectors: bfloat16 [8, 131072], P(None, ('row', 'col')), may hold values from -6 to 6
Outputs:
- basis: float32 [8, 131072], P(None, ('row', 'col'))
The draws below stay inside these ranges and needn't reach their ends.
All inputs are finite; a program needn't handle non-finite values.
Results may differ from the reference program's by a relative error of at most 0.012.
Values may be sent and summed in bfloat16 or wider, within the bound.
A program may use at most 64 MiB of HBM per device.

```python
import math
import jax
import jax.numpy as jnp
from jax import lax

DIM = 16
KVEC = 8
NPTS = 131072


def shard_levels(stream_key, extent, shards, least, largest):
    factor_of, own = 1.0, jax.random.fold_in(stream_key, 6)
    for position, blocks in shards:
        heights = jnp.exp(jax.random.uniform(jax.random.fold_in(own, position), (blocks,), jnp.float32, least / len(shards), largest / len(shards)))
        factor_of = factor_of * jnp.repeat(heights, extent[position] // blocks).reshape([-1 if axis == position else 1 for axis in range(len(extent))])
    return factor_of


def gaussian(rng, dims, width, reach, shards=(), dtype=jnp.bfloat16):
    drawn = jax.random.normal(rng, dims, jnp.float32) * width
    if len(shards) > 0:
        drawn = shard_levels(rng, dims, shards, -0.22, 0.18) * drawn
    return jnp.clip(drawn, min=-reach, max=reach).astype(dtype)


def setup_inputs(seed: int = 0) -> dict:
    splits = jax.random.split(jax.random.key(seed), 4)
    return {
        "points": gaussian(splits[0], (DIM, NPTS), 1.0, 6.0, ((1, 256),)),
        "spread": jnp.clip(jnp.exp(math.log(12.0) - 1.7917595 * jax.random.uniform(splits[1], (NPTS,), jnp.float32) ** shard_levels(splits[1], (NPTS,), ((0, 256),), -0.2, 0.2)), 2.0, 12.0).astype(jnp.bfloat16),
        "vectors": gaussian(splits[2], (KVEC, NPTS), 1.0, 6.0, ((1, 256),)),
    }


def reference(points, spread, vectors):
    count = points.shape[1]
    ones_row = jnp.ones((1, count), jnp.bfloat16)
    extended = jnp.concatenate([vectors, ones_row], axis=0)
    sqnorm = lax.optimization_barrier(jnp.sum(points.astype(jnp.float32) * points.astype(jnp.float32), axis=0))
    scales = spread.astype(jnp.float32)
    block = math.gcd(count, 512)
    nblocks = count // block
    row_pts = jnp.transpose(points.reshape(points.shape[0], nblocks, block), (1, 0, 2))
    row_norm = sqnorm.reshape(nblocks, block)
    row_scale = scales.reshape(nblocks, block)

    def one_block(operands):
        pts_blk, norm_blk, scale_blk = operands
        cross = lax.dot_general(pts_blk.astype(jnp.float32), points.astype(jnp.float32), (((0,), (0,)), ((), ())), preferred_element_type=jnp.float32)
        dist = norm_blk[:, None] + sqnorm[None, :] - 2.0 * cross
        affinity = jnp.exp(-dist / (scale_blk[:, None] * scales[None, :])).astype(jnp.bfloat16)
        return lax.dot_general(extended.astype(jnp.float32), affinity.astype(jnp.float32), (((1,), (1,)), ((), ())), preferred_element_type=jnp.float32)
    parts = lax.map(one_block, (row_pts, row_norm, row_scale))
    product = jnp.transpose(parts, (1, 0, 2)).reshape(extended.shape[0], count)
    kvec = vectors.shape[0]
    update = product[:kvec] / product[kvec:kvec + 1]
    gram = lax.optimization_barrier(jnp.sum(update[:, None, :] * update[None, :, :], axis=2))
    lower = jnp.linalg.cholesky(gram)
    solved = lax.linalg.triangular_solve(lower, update, left_side=True, lower=True)
    return jnp.sqrt(jnp.float32(count)) * solved
```

```python
import functools
import math

import jax
import jax.numpy as jnp
from jax import lax
from jax.experimental import pallas as pl
from jax.experimental.pallas import tpu as pltpu
from jax.sharding import PartitionSpec as P

F32, BF16 = jnp.float32, jnp.bfloat16
MESH = pl.DeviceIdType.MESH
LOG2E = 1.4426950408889634
DEPTH = 128
PAD = 16
PIECES_LEFT = (0, 0, 1, 1, 0, 2)
PIECES_RIGHT = (0, 1, 0, 1, 2, 0)


def split3(x):
    high = x.astype(BF16)
    rest = x - high.astype(F32)
    mid = rest.astype(BF16)
    low = (rest - mid.astype(F32)).astype(BF16)
    return high, mid, low


def factor(block, left):
    pts = block[:16].astype(F32)
    tail = block[16:].astype(F32)
    inv = 1.0 / tail[9:10]
    w = pts * inv
    norm = jnp.sum(pts * pts, axis=0, keepdims=True) * inv
    if left:
        w = w * (2.0 * LOG2E)
        terms = (norm * -LOG2E, inv * -LOG2E)
        order = PIECES_LEFT
    else:
        terms = (inv, norm)
        order = PIECES_RIGHT
    pieces = split3(w)
    rows = lax.broadcasted_iota(jnp.int32, pts.shape, 0)
    extra = jnp.zeros_like(pts)
    for t, term in enumerate(terms):
        cut = split3(term)
        for k, p in enumerate(order):
            extra = jnp.where(rows == 6 * t + k, cut[p].astype(F32), extra)
    return jnp.concatenate(
        [pieces[p] for p in order] + [extra.astype(BF16), jnp.zeros(pts.shape, BF16)], axis=0
    )


def kernel(n_row, n_col, pts_ref, spread_ref, vec_ref, out_ref, own, got_r, got_c, right, left, part_r, part_c,
           in_r, in_c, gram, gsend, sems):
    half_r, half_c = n_row // 2, n_col // 2
    r, c = lax.axis_index("row"), lax.axis_index("col")
    local = pts_ref.shape[1]

    def at_row(d):
        return (lax.rem(r + d + n_row, n_row), c)

    def at_col(d):
        return (r, lax.rem(c + d + n_col, n_col))

    barrier = pltpu.get_barrier_semaphore()
    for d in range(1, n_row):
        pl.semaphore_signal(barrier, inc=1, device_id=at_row(d), device_id_type=MESH)
    for d in range(1, n_col):
        pl.semaphore_signal(barrier, inc=1, device_id=at_col(d), device_id_type=MESH)

    own[:16, :] = pts_ref[...]
    rows8 = lax.broadcasted_iota(jnp.int32, (8, local), 0)
    tail = jnp.where(rows8 == 0, 1.0, jnp.where(rows8 == 1, spread_ref[...].astype(F32), 0.0))
    own[16:, :] = jnp.concatenate([vec_ref[...].astype(F32), tail], axis=0).astype(BF16)

    pl.semaphore_wait(barrier, n_row + n_col - 2)

    def copy(src, dst, name, slot, device):
        send, recv = sems[name]
        return pltpu.make_async_remote_copy(
            src_ref=src, dst_ref=dst.at[slot], send_sem=send.at[slot], recv_sem=recv.at[slot],
            device_id=device, device_id_type=MESH)

    gets_c = {d: copy(own, got_c, "gather_c", d, at_row(-d)) for d in range(1, half_r + 1)}
    gets_r = {d: copy(own, got_r, "gather_r", d, at_col(-d)) for d in range(1, n_col)}
    for d in range(1, n_col):
        gets_r[d].start()
        if d in gets_c:
            gets_c[d].start()
    for d in range(n_col, half_r + 1):
        gets_c[d].start()
    got_r[0] = own[...]
    got_c[0] = own[...]

    part_r[...] = jnp.zeros_like(part_r)
    part_c[...] = jnp.zeros_like(part_c)
    for d in gets_r:
        gets_r[d].wait_recv()
    for d in gets_c:
        gets_c[d].wait_recv()

    def make_right(d, _):
        right[d] = factor(got_r[d], False)
        return 0

    def make_left(d, _):
        left[d] = jnp.transpose(factor(got_c[d], True))
        return 0

    lax.fori_loop(0, n_col, make_right, 0)
    lax.fori_loop(0, half_r + 1, make_left, 0)

    def pair(dr, dc, both):
        expo = jnp.dot(left[dr], right[dc], preferred_element_type=F32)
        affinity = jnp.exp2(expo).astype(BF16)
        part_r[dc] += jnp.dot(got_c[dr, 16:, :], affinity, preferred_element_type=F32)
        if both:
            part_c[dr] += lax.dot_general(
                got_r[dc, 16:, :], affinity, (((1,), (1,)), ((), ())), preferred_element_type=F32)

    def both_pair(dr):
        def step(dc, _):
            pair(dr, dc, True)
            return 0
        return step

    puts_r = {d: copy(part_r.at[d], in_r, "reduce_r", d, at_col(d)) for d in range(1, n_col)}
    puts_c = {d: copy(part_c.at[d], in_c, "reduce_c", d, at_row(d)) for d in range(1, half_r + 1)}

    for dr in (0, half_r):
        pair(dr, 0, False)
        pair(dr, half_c, False)
        lax.fori_loop(1, half_c, both_pair(dr), 0, unroll=True)
        if dr:
            puts_c[dr].start()

    def middle(dr, _):
        lax.fori_loop(0, n_col, both_pair(dr), 0, unroll=True)
        copy(part_c.at[dr], in_c, "reduce_c", dr, at_row(dr)).start()
        return 0

    lax.fori_loop(1, half_r, middle, 0)
    for d in puts_r:
        puts_r[d].start()
    total = part_r[0] + part_c[0]
    for d in puts_c:
        puts_c[d].wait_recv()
        total += in_c[d]
    for d in puts_r:
        puts_r[d].wait_recv()
        total += in_r[d]
    update = total[:8] / total[8:9]
    mine = lax.dot_general(
        update, update, (((1,), (1,)), ((), ())), precision=lax.Precision.HIGHEST, preferred_element_type=F32)

    pending = []
    gsend[...] = jnp.zeros_like(gsend)
    for stage, (count, place) in enumerate(((n_col, at_col), (n_row, at_row))):
        gsend[stage, :, :8] = mine
        puts = [copy(gsend.at[stage], gram.at[stage], ("gram_c", "gram_r")[stage], d, place(d)) for d in range(1, count)]
        for p in puts:
            p.start()
        acc = gsend[stage]
        for d, p in enumerate(puts, 1):
            p.wait_recv()
            acc += gram[stage, d]
        mine = acc[:, :8]
        pending += puts

    g, u = mine, update
    rows_g = lax.broadcasted_iota(jnp.int32, g.shape, 0)
    rows_u = lax.broadcasted_iota(jnp.int32, u.shape, 0)
    for k in range(8):
        scale = 1.0 / jnp.sqrt(g[k : k + 1, k : k + 1])
        row_g, row_u = g[k : k + 1] * scale, u[k : k + 1] * scale
        col = g[:, k : k + 1] * scale
        u = jnp.where(rows_u == k, row_u, jnp.where(rows_u > k, u - col * row_u, u))
        g = jnp.where(rows_g > k, g - col * row_g, g)
    out_ref[...] = u * math.sqrt(local * n_row * n_col)

    for group in (gets_r, gets_c, puts_r, puts_c):
        for p in group.values():
            p.wait_send()
    for p in pending:
        p.wait_send()


def run(n_row, n_col, *refs):
    refs, flat = refs[:-12], refs[-12:]
    names = ("gather_r", "gather_c", "reduce_r", "reduce_c", "gram_c", "gram_r")
    sems = {name: (flat[2 * i], flat[2 * i + 1]) for i, name in enumerate(names)}
    kernel(n_row, n_col, *refs, sems)


def solution(mesh):
    n_row, n_col = mesh.shape["row"], mesh.shape["col"]
    half_r = n_row // 2

    def shards(points, spread, vectors):
        local = points.shape[1]
        vmem = pl.BlockSpec(memory_space=pltpu.VMEM)
        counts = (n_col, half_r + 1, n_col, half_r + 1, n_col, n_row)
        most = max(n_row, n_col)
        return pl.pallas_call(
            functools.partial(run, n_row, n_col),
            out_shape=jax.ShapeDtypeStruct((8, local), F32),
            in_specs=[vmem] * 3,
            out_specs=vmem,
            scratch_shapes=[
                pltpu.VMEM((32, local), BF16),
                pltpu.VMEM((n_col, 32, local), BF16),
                pltpu.VMEM((half_r + 1, 32, local), BF16),
                pltpu.VMEM((n_col, DEPTH, local), BF16),
                pltpu.VMEM((half_r + 1, local, DEPTH), BF16),
                pltpu.VMEM((n_col, PAD, local), F32),
                pltpu.VMEM((half_r + 1, PAD, local), F32),
                pltpu.VMEM((n_col, PAD, local), F32),
                pltpu.VMEM((half_r + 1, PAD, local), F32),
                pltpu.VMEM((2, most, 8, 128), F32),
                pltpu.VMEM((2, 8, 128), F32),
            ] + [pltpu.SemaphoreType.DMA((n,)) for n in counts for _ in range(2)],
            compiler_params=pltpu.CompilerParams(
                collective_id=0, has_side_effects=True, vmem_limit_bytes=48 << 20),
            name="subspace",
        )(points, spread.reshape(1, local), vectors)

    in_specs = (P(None, ("row", "col")), P(("row", "col")), P(None, ("row", "col")))
    return jax.shard_map(shards, mesh=mesh, in_specs=in_specs, out_specs=P(None, ("row", "col")), check_vma=False)
```

```python
import functools
import math

import jax
import jax.numpy as jnp
from jax import lax
from jax.experimental import pallas as pl
from jax.experimental.pallas import tpu as pltpu
from jax.sharding import PartitionSpec as P

F32, BF16 = jnp.float32, jnp.bfloat16
MESH = pl.DeviceIdType.MESH
LOG2E = 1.4426950408889634
DEPTH = 128
PAD = 16
PIECES_LEFT = (0, 0, 1, 1, 0, 2)
PIECES_RIGHT = (0, 1, 0, 1, 2, 0)


def split3(x):
    high = x.astype(BF16)
    rest = x - high.astype(F32)
    mid = rest.astype(BF16)
    low = (rest - mid.astype(F32)).astype(BF16)
    return high, mid, low


def factor(block, left):
    pts = block[:16].astype(F32)
    tail = block[16:].astype(F32)
    inv = 1.0 / tail[9:10]
    w = pts * inv
    norm = jnp.sum(pts * pts, axis=0, keepdims=True) * inv
    if left:
        w = w * (2.0 * LOG2E)
        terms = (norm * -LOG2E, inv * -LOG2E)
        order = PIECES_LEFT
    else:
        terms = (inv, norm)
        order = PIECES_RIGHT
    pieces = split3(w)
    rows = lax.broadcasted_iota(jnp.int32, pts.shape, 0)
    extra = jnp.zeros_like(pts)
    for t, term in enumerate(terms):
        cut = split3(term)
        for k, p in enumerate(order):
            extra = jnp.where(rows == 6 * t + k, cut[p].astype(F32), extra)
    return jnp.concatenate(
        [pieces[p] for p in order] + [extra.astype(BF16), jnp.zeros(pts.shape, BF16)], axis=0
    )


def kernel(n_row, n_col, pts_ref, spread_ref, vec_ref, out_ref, own, spread_v, vec_v, got_r, got_c, right, left,
           part_r, part_c, out_r, out_c, in_r, in_c, gram, gsend, aff, aff_t, load_sem, sems):
    half_r, half_c = n_row // 2, n_col // 2
    chunks = own.shape[1] // 128
    r, c = lax.axis_index("row"), lax.axis_index("col")
    local = own.shape[1]

    def at_row(d):
        return (lax.rem(r + d + n_row, n_row), c)

    def at_col(d):
        return (r, lax.rem(c + d + n_col, n_col))

    barrier = pltpu.get_barrier_semaphore()
    for d in range(1, n_col):
        pl.semaphore_signal(barrier, inc=1, device_id=at_col(d), device_id_type=MESH)
    for d in range(1, n_row):
        pl.semaphore_signal(barrier, inc=1, device_id=at_row(d), device_id_type=MESH)

    loads = [
        pltpu.make_async_copy(pts_ref, own.at[:16, :], load_sem.at[0]),
        pltpu.make_async_copy(vec_ref, vec_v, load_sem.at[1]),
        pltpu.make_async_copy(spread_ref, spread_v, load_sem.at[2]),
    ]
    for load in loads:
        load.start()
    part_r[...] = jnp.zeros_like(part_r)
    part_c[...] = jnp.zeros_like(part_c)
    gsend[...] = jnp.zeros_like(gsend)
    for load in loads:
        load.wait()
    rows8 = lax.broadcasted_iota(jnp.int32, (8, local), 0)
    spread = spread_v[...].astype(F32).reshape(1, local)
    tail = jnp.where(rows8 == 0, 1.0, jnp.where(rows8 == 1, spread, 0.0))
    own[16:, :] = jnp.concatenate([vec_v[...].astype(F32), tail], axis=0).astype(BF16)
    got_r[0] = own[...]
    got_c[0] = own[...]

    def copy(src, dst, name, slot, device):
        send, recv = sems[name]
        return pltpu.make_async_remote_copy(
            src_ref=src, dst_ref=dst.at[slot], send_sem=send.at[slot], recv_sem=recv.at[slot],
            device_id=device, device_id_type=MESH)

    def get_r(d):
        return copy(own, got_r, "gather_r", d, at_col(-d))

    def get_c(d):
        return copy(own, got_c, "gather_c", d, at_row(-d))

    def put_r(d):
        return copy(out_r.at[d], in_r, "reduce_r", d, at_col(d))

    def put_c(d):
        return copy(out_c.at[d], in_c, "reduce_c", d, at_row(d))

    def pack(dst, src):
        for n in range(chunks):
            lanes = pl.ds(128 * n, 128)
            dst[pl.ds(8 * n, 8), :] = src[:8, lanes]
            dst[pl.ds(8 * chunks + n, 1), :] = src[8:9, lanes]

    def add(totals, packed):
        product, degree = totals
        parts = [packed[pl.ds(8 * n, 8), :] for n in range(chunks)]
        degrees = packed[pl.ds(8 * chunks, chunks), :]
        return tuple(a + b for a, b in zip(product, parts)), degree + degrees

    def send_r(d):
        pack(out_r.at[d], part_r.at[d])
        put_r(d).start()

    def send_c(d):
        pack(out_c.at[d], part_c.at[d])
        put_c(d).start()

    def make_right(d):
        right[d] = factor(got_r[d], False)

    def make_left(d):
        left[d] = jnp.transpose(factor(got_c[d], True))

    def take_r(d):
        get_r(d).wait_recv()
        make_right(d)

    def take_c(d):
        get_c(d).wait_recv()
        make_left(d)

    def produce(slot, dr, dc, both=True):
        expo = jnp.dot(left[dr], right[dc], preferred_element_type=F32)
        affinity = jnp.exp2(expo).astype(BF16)
        aff[slot] = affinity
        if both:
            aff_t[slot] = jnp.transpose(affinity)

    def consume(slot, dr, dc, both=True):
        part_r[dc] += jnp.dot(got_c[dr, 16:, :], aff[slot], preferred_element_type=F32)
        if both:
            part_c[dr] += jnp.dot(got_r[dc, 16:, :], aff_t[slot], preferred_element_type=F32)

    make_right(0)
    make_left(0)
    produce(0, 0, 0, False)

    pl.semaphore_wait(barrier, n_row + n_col - 2)
    for d in range(1, half_c + 1):
        get_r(d).start()
    for d in range(1, half_r):
        get_c(d).start()
    for d in range(half_c + 1, n_col):
        get_r(d).start()
    get_c(half_r).start()

    for d in range(1, half_c + 1):
        take_r(d)
        produce(d % 2, 0, d, d < half_c)
        consume((d - 1) % 2, 0, d - 1, d > 1)
    take_c(1)
    produce((half_c + 1) % 2, 1, 0)
    consume(half_c % 2, 0, half_c, False)

    passes = half_r - 1

    def middle(t, _):
        far = t // passes
        dr = 1 + t - far * passes
        base = far * half_c
        after = t + 1
        far_after = after // passes
        last = after == 2 * passes
        dr_after = jnp.where(last, half_r, 1 + after - far_after * passes)
        base_after = jnp.where(last, half_c, far_after * half_c)

        @pl.when(t < passes - 1)
        def _():
            take_c(dr + 1)

        @pl.when(t == passes - 1)
        def _():
            for d in range(half_c + 1, n_col):
                take_r(d)
            take_c(half_r)

        @pl.when(t > passes + 1)
        def _():
            send_c(t - passes - 1)

        for k in range(half_c):
            slot = (half_c + 1 + k) % 2
            if k < half_c - 1:
                produce(1 - slot, dr, base + k + 1)
            else:
                produce(1 - slot, dr_after, base_after)
            consume(slot, dr, base + k)
        return 0

    lax.fori_loop(0, 2 * passes, middle, 0)
    for d in range(max(1, passes - 1), passes + 1):
        send_c(d)
    for d in range(half_c + 1, n_col):
        send_r(d)

    order = [half_c, 0] + list(range(1, half_c))
    for n, d in enumerate(order):
        slot = (half_c + 1 + n) % 2
        if n + 1 < len(order):
            produce(1 - slot, half_r, order[n + 1], n >= 1)
        consume(slot, half_r, d, n >= 2)
        if d:
            send_r(d)
    send_c(half_r)

    part_r[0] += part_c[0]
    pack(out_r.at[0], part_r.at[0])
    totals = (tuple(jnp.zeros((8, 128), F32) for _ in range(chunks)), jnp.zeros((chunks, 128), F32))
    totals = add(totals, out_r.at[0])
    for d in range(1, half_r):
        put_c(d).wait_recv()
        totals = add(totals, in_c.at[d])
    for d in list(range(half_c + 1, n_col)) + order:
        if d:
            put_r(d).wait_recv()
            totals = add(totals, in_r.at[d])
    put_c(half_r).wait_recv()
    product, degree = add(totals, in_c.at[half_r])
    update = jnp.concatenate([product[n] / degree[n : n + 1] for n in range(chunks)], axis=1)
    mine = lax.dot_general(
        update, update, (((1,), (1,)), ((), ())), precision=lax.Precision.HIGHEST, preferred_element_type=F32)

    pending = []
    for stage, (count, place) in enumerate(((n_col, at_col), (n_row, at_row))):
        gsend[stage, :, :8] = mine
        puts = [copy(gsend.at[stage], gram.at[stage], ("gram_c", "gram_r")[stage], d, place(d)) for d in range(1, count)]
        for p in puts:
            p.start()
        acc = gsend[stage]
        for d, p in enumerate(puts, 1):
            p.wait_recv()
            acc += gram[stage, d]
        mine = acc[:, :8]
        pending += puts

    g, u = mine, update
    rows_g = lax.broadcasted_iota(jnp.int32, g.shape, 0)
    rows_u = lax.broadcasted_iota(jnp.int32, u.shape, 0)
    for k in range(8):
        scale = 1.0 / jnp.sqrt(g[k : k + 1, k : k + 1])
        row_g, row_u = g[k : k + 1] * scale, u[k : k + 1] * scale
        col = g[:, k : k + 1] * scale
        u = jnp.where(rows_u == k, row_u, jnp.where(rows_u > k, u - col * row_u, u))
        g = jnp.where(rows_g > k, g - col * row_g, g)
    out_ref[...] = u * math.sqrt(local * n_row * n_col)

    for d in range(1, n_col):
        get_r(d).wait_send()
        put_r(d).wait_send()
    for d in range(1, half_r + 1):
        get_c(d).wait_send()
        put_c(d).wait_send()
    for p in pending:
        p.wait_send()


def run(n_row, n_col, *refs):
    refs, flat = refs[:-12], refs[-12:]
    names = ("gather_r", "gather_c", "reduce_r", "reduce_c", "gram_c", "gram_r")
    sems = {name: (flat[2 * i], flat[2 * i + 1]) for i, name in enumerate(names)}
    kernel(n_row, n_col, *refs, sems)


def solution(mesh):
    n_row, n_col = mesh.shape["row"], mesh.shape["col"]
    half_r = n_row // 2

    def shards(points, spread, vectors):
        local = points.shape[1]
        vmem = pl.BlockSpec(memory_space=pltpu.VMEM)
        counts = (n_col, half_r + 1, n_col, half_r + 1, n_col, n_row)
        most = max(n_row, n_col)
        packed = -(-9 * (local // 128) // 8) * 8
        return pl.pallas_call(
            functools.partial(run, n_row, n_col),
            out_shape=jax.ShapeDtypeStruct((8, local), F32),
            in_specs=[pl.BlockSpec(memory_space=pl.ANY)] * 3,
            out_specs=vmem,
            scratch_shapes=[
                pltpu.VMEM((32, local), BF16),
                pltpu.VMEM((local,), BF16),
                pltpu.VMEM((8, local), BF16),
                pltpu.VMEM((n_col, 32, local), BF16),
                pltpu.VMEM((half_r + 1, 32, local), BF16),
                pltpu.VMEM((n_col, DEPTH, local), BF16),
                pltpu.VMEM((half_r + 1, local, DEPTH), BF16),
                pltpu.VMEM((n_col, PAD, local), F32),
                pltpu.VMEM((half_r + 1, PAD, local), F32),
                pltpu.VMEM((n_col, packed, 128), F32),
                pltpu.VMEM((half_r + 1, packed, 128), F32),
                pltpu.VMEM((n_col, packed, 128), F32),
                pltpu.VMEM((half_r + 1, packed, 128), F32),
                pltpu.VMEM((2, most, 8, 128), F32),
                pltpu.VMEM((2, 8, 128), F32),
                pltpu.VMEM((2, local, local), BF16),
                pltpu.VMEM((2, local, local), BF16),
                pltpu.SemaphoreType.DMA((3,)),
            ] + [pltpu.SemaphoreType.DMA((n,)) for n in counts for _ in range(2)],
            compiler_params=pltpu.CompilerParams(
                collective_id=0, has_side_effects=True, vmem_limit_bytes=48 << 20),
            name="subspace",
        )(points, spread, vectors)

    in_specs = (P(None, ("row", "col")), P(("row", "col")), P(None, ("row", "col")))
    return jax.shard_map(shards, mesh=mesh, in_specs=in_specs, out_specs=P(None, ("row", "col")), check_vma=False)
```

```python
import functools
import math

import jax
import jax.numpy as jnp
from jax import lax
from jax.experimental import pallas as pl
from jax.experimental.pallas import tpu as pltpu
from jax.sharding import PartitionSpec as P

F32, BF16 = jnp.float32, jnp.bfloat16
MESH = pl.DeviceIdType.MESH
LOG2E = 1.4426950408889634
DEPTH = 128
PAD = 16
PIECES_LEFT = (0, 0, 1, 1, 0, 2)
PIECES_RIGHT = (0, 1, 0, 1, 2, 0)


def split3(x):
    high = x.astype(BF16)
    rest = x - high.astype(F32)
    mid = rest.astype(BF16)
    low = (rest - mid.astype(F32)).astype(BF16)
    return high, mid, low


def factor(block, left):
    pts = block[:16].astype(F32)
    tail = block[16:].astype(F32)
    inv = 1.0 / tail[9:10]
    w = pts * inv
    norm = jnp.sum(pts * pts, axis=0, keepdims=True) * inv
    if left:
        w = w * (2.0 * LOG2E)
        terms = (norm * -LOG2E, inv * -LOG2E)
        order = PIECES_LEFT
    else:
        terms = (inv, norm)
        order = PIECES_RIGHT
    pieces = split3(w)
    rows = lax.broadcasted_iota(jnp.int32, pts.shape, 0)
    extra = jnp.zeros_like(pts)
    for t, term in enumerate(terms):
        cut = split3(term)
        for k, p in enumerate(order):
            extra = jnp.where(rows == 6 * t + k, cut[p].astype(F32), extra)
    return jnp.concatenate(
        [pieces[p] for p in order] + [extra.astype(BF16), jnp.zeros(pts.shape, BF16)], axis=0
    )


def kernel(n_row, n_col, pts_ref, spread_ref, vec_ref, out_ref, own, spread_v, vec_v, got_r, got_c, right, left,
           part_r, part_c, out_r, out_c, in_r, in_c, gram, gsend, aff, aff_t, load_sem, sems):
    half_r, half_c = n_row // 2, n_col // 2
    chunks = own.shape[1] // 128
    r, c = lax.axis_index("row"), lax.axis_index("col")
    local = own.shape[1]

    def at_row(d):
        return (lax.rem(r + d + n_row, n_row), c)

    def at_col(d):
        return (r, lax.rem(c + d + n_col, n_col))

    barrier = pltpu.get_barrier_semaphore()
    for d in range(1, n_col):
        pl.semaphore_signal(barrier, inc=1, device_id=at_col(d), device_id_type=MESH)
    for d in range(1, n_row):
        pl.semaphore_signal(barrier, inc=1, device_id=at_row(d), device_id_type=MESH)

    loads = [
        pltpu.make_async_copy(pts_ref, own.at[:16, :], load_sem.at[0]),
        pltpu.make_async_copy(vec_ref, vec_v, load_sem.at[1]),
        pltpu.make_async_copy(spread_ref, spread_v, load_sem.at[2]),
    ]
    for load in loads:
        load.start()
    part_r[...] = jnp.zeros_like(part_r)
    part_c[...] = jnp.zeros_like(part_c)
    gsend[...] = jnp.zeros_like(gsend)
    for load in loads:
        load.wait()
    rows8 = lax.broadcasted_iota(jnp.int32, (8, local), 0)
    spread = spread_v[...].astype(F32).reshape(1, local)
    tail = jnp.where(rows8 == 0, 1.0, jnp.where(rows8 == 1, spread, 0.0))
    own[16:, :] = jnp.concatenate([vec_v[...].astype(F32), tail], axis=0).astype(BF16)
    got_r[0] = own[...]
    got_c[0] = own[...]

    def copy(src, dst, name, slot, device):
        send, recv = sems[name]
        return pltpu.make_async_remote_copy(
            src_ref=src, dst_ref=dst.at[slot], send_sem=send.at[slot], recv_sem=recv.at[slot],
            device_id=device, device_id_type=MESH)

    def get_r(d):
        return copy(own, got_r, "gather_r", d, at_col(-d))

    def get_c(d):
        return copy(own, got_c, "gather_c", d, at_row(-d))

    def put_r(d):
        return copy(out_r.at[d], in_r, "reduce_r", d, at_col(d))

    def put_c(d):
        return copy(out_c.at[d], in_c, "reduce_c", d, at_row(d))

    def pack(dst, src):
        for n in range(chunks):
            lanes = pl.ds(128 * n, 128)
            dst[pl.ds(8 * n, 8), :] = src[:8, lanes]
            dst[pl.ds(8 * chunks + n, 1), :] = src[8:9, lanes]

    def add(totals, packed):
        product, degree = totals
        parts = [packed[pl.ds(8 * n, 8), :] for n in range(chunks)]
        degrees = packed[pl.ds(8 * chunks, chunks), :]
        return tuple(a + b for a, b in zip(product, parts)), degree + degrees

    def send_r(d):
        pack(out_r.at[d], part_r.at[d])
        put_r(d).start()

    def send_c(d):
        pack(out_c.at[d], part_c.at[d])
        put_c(d).start()

    def make_right(d):
        right[d] = factor(got_r[d], False)

    def make_left(d):
        left[d] = jnp.transpose(factor(got_c[d], True))

    def take_r(d):
        get_r(d).wait_recv()
        make_right(d)

    def take_c(d):
        get_c(d).wait_recv()
        make_left(d)

    half = local // 2

    def produce_part(slot, dr, dc, both, rows, lanes):
        expo = jnp.dot(left[dr, rows, :], right[dc, :, lanes], preferred_element_type=F32)
        affinity = jnp.exp2(expo).astype(BF16)
        aff[slot, rows, lanes] = affinity
        if both:
            aff_t[slot, lanes, rows] = jnp.transpose(affinity)

    def use_columns(slot, dr, dc, lanes):
        part_r[dc, :, lanes] += jnp.dot(got_c[dr, 16:, :], aff[slot, :, lanes], preferred_element_type=F32)

    def use_rows(slot, dr, dc, rows):
        part_c[dr, :, rows] += jnp.dot(got_r[dc, 16:, :], aff_t[slot, :, rows], preferred_element_type=F32)

    def step(cur, after):
        for q in range(4):
            rows, lanes = pl.ds((q // 2) * half, half), pl.ds((q % 2) * half, half)
            if after is not None:
                produce_part(*after, rows, lanes)
            if cur is not None:
                slot, dr, dc, both = cur
                part = pl.ds((q % 2) * half, half)
                if q < 2:
                    use_columns(slot, dr, dc, part)
                elif both:
                    use_rows(slot, dr, dc, part)

    make_right(0)
    make_left(0)
    step(None, (0, 0, 0, False))

    pl.semaphore_wait(barrier, n_row + n_col - 2)
    for d in range(1, half_c + 1):
        get_r(d).start()
    get_c(1).start()
    far_r = range(half_c + 1, n_col)

    for d in range(1, half_c + 1):
        if 1 < d < half_r:
            get_c(d).start()
        take_r(d)
        step(((d - 1) % 2, 0, d - 1, d > 1), (d % 2, 0, d, d < half_c))
    for d in range(half_c + 1, half_r):
        get_c(d).start()
    done = half_c + 1
    take_c(1)
    step((1 - done % 2, 0, half_c, False), (done % 2, 1, 0, True))

    def near(t, _):
        dr = t + 1

        @pl.when(t == 0)
        def _():
            for d in far_r:
                get_r(d).start()
            get_c(half_r).start()

        @pl.when(t < half_r - 2)
        def _():
            take_c(dr + 1)

        @pl.when(t == half_r - 2)
        def _():
            take_c(half_r)

        wrap = t == half_r - 2
        dr_after = dr + 1
        dc_after = jnp.where(wrap, half_c, 0)
        for k in range(half_c):
            slot = (done + k) % 2
            after = (dr, k + 1) if k < half_c - 1 else (dr_after, dc_after)
            step((slot, dr, k, True), (1 - slot, *after, True))
        return 0

    lax.fori_loop(0, half_r - 1, near, 0)
    done += (half_r - 1) * half_c

    for d in far_r:
        take_r(d)
    order = [half_c, 0] + list(range(1, half_c))
    for n, d in enumerate(order):
        slot = (done + n) % 2
        after = (half_r, order[n + 1], n >= 1) if n + 1 < len(order) else (1, half_c, True)
        step((slot, half_r, d, n >= 2), (1 - slot, *after))
    done += len(order)
    send_c(half_r)
    for d in range(1, half_c):
        send_r(d)

    def far(t, last):
        dc = half_c + 2 * t
        pairs = [(dc + e, dr) for e in range(2) for dr in range(1, half_r)]
        if not last:
            @pl.when(t > 0)
            def _():
                send_r(dc - 2)
                send_r(dc - 1)
        elif half_c > 2:
            send_r(dc - 2)
            send_r(dc - 1)
        for n, (d, dr) in enumerate(pairs):
            slot = (done + n) % 2
            after = None
            if n + 1 < len(pairs):
                after = (1 - slot, pairs[n + 1][1], pairs[n + 1][0], True)
            elif not last:
                after = (1 - slot, 1, dc + 2, True)
            step((slot, dr, d, True), after)
            if last and n == half_r - 2:
                send_r(d)
            if last and n >= half_r - 1:
                send_c(dr)
        if last:
            send_r(dc + 1)
        return 0

    lax.fori_loop(0, half_c // 2 - 1, lambda t, _: far(t, False), 0)
    far(half_c // 2 - 1, True)

    part_r[0] += part_c[0]
    pack(out_r.at[0], part_r.at[0])
    totals = (tuple(jnp.zeros((8, 128), F32) for _ in range(chunks)), jnp.zeros((chunks, 128), F32))
    totals = add(totals, out_r.at[0])
    put_c(half_r).wait_recv()
    totals = add(totals, in_c.at[half_r])
    for d in range(1, n_col - 1):
        put_r(d).wait_recv()
        totals = add(totals, in_r.at[d])
    for d in range(1, half_r):
        put_c(d).wait_recv()
        totals = add(totals, in_c.at[d])
    put_r(n_col - 1).wait_recv()
    product, degree = add(totals, in_r.at[n_col - 1])
    update = jnp.concatenate([product[n] / degree[n : n + 1] for n in range(chunks)], axis=1)
    mine = lax.dot_general(
        update, update, (((1,), (1,)), ((), ())), precision=lax.Precision.HIGHEST, preferred_element_type=F32)

    pending = []
    for stage, (count, place) in enumerate(((n_col, at_col), (n_row, at_row))):
        gsend[stage, :, :8] = mine
        puts = [copy(gsend.at[stage], gram.at[stage], ("gram_c", "gram_r")[stage], d, place(d)) for d in sorted(range(1, count), key=lambda d: -min(d % 8, 8 - d % 8))]
        for p in puts:
            p.start()
        acc = gsend[stage]
        for p in puts:
            p.wait_recv()
        for d in range(1, count):
            acc += gram[stage, d]
        mine = acc[:, :8]
        pending += puts

    g, u = mine, update
    rows_g = lax.broadcasted_iota(jnp.int32, g.shape, 0)
    rows_u = lax.broadcasted_iota(jnp.int32, u.shape, 0)
    for k in range(8):
        scale = 1.0 / jnp.sqrt(g[k : k + 1, k : k + 1])
        row_g, row_u = g[k : k + 1] * scale, u[k : k + 1] * scale
        col = g[:, k : k + 1] * scale
        u = jnp.where(rows_u == k, row_u, jnp.where(rows_u > k, u - col * row_u, u))
        g = jnp.where(rows_g > k, g - col * row_g, g)
    out_ref[...] = u * math.sqrt(local * n_row * n_col)

    for d in range(1, n_col):
        get_r(d).wait_send()
        put_r(d).wait_send()
    for d in range(1, half_r + 1):
        get_c(d).wait_send()
        put_c(d).wait_send()
    for p in pending:
        p.wait_send()


def run(n_row, n_col, *refs):
    refs, flat = refs[:-12], refs[-12:]
    names = ("gather_r", "gather_c", "reduce_r", "reduce_c", "gram_c", "gram_r")
    sems = {name: (flat[2 * i], flat[2 * i + 1]) for i, name in enumerate(names)}
    kernel(n_row, n_col, *refs, sems)


def solution(mesh):
    n_row, n_col = mesh.shape["row"], mesh.shape["col"]
    half_r = n_row // 2

    def shards(points, spread, vectors):
        local = points.shape[1]
        vmem = pl.BlockSpec(memory_space=pltpu.VMEM)
        counts = (n_col, half_r + 1, n_col, half_r + 1, n_col, n_row)
        most = max(n_row, n_col)
        packed = -(-9 * (local // 128) // 8) * 8
        return pl.pallas_call(
            functools.partial(run, n_row, n_col),
            out_shape=jax.ShapeDtypeStruct((8, local), F32),
            in_specs=[pl.BlockSpec(memory_space=pl.ANY)] * 3,
            out_specs=vmem,
            scratch_shapes=[
                pltpu.VMEM((32, local), BF16),
                pltpu.VMEM((local,), BF16),
                pltpu.VMEM((8, local), BF16),
                pltpu.VMEM((n_col, 32, local), BF16),
                pltpu.VMEM((half_r + 1, 32, local), BF16),
                pltpu.VMEM((n_col, DEPTH, local), BF16),
                pltpu.VMEM((half_r + 1, local, DEPTH), BF16),
                pltpu.VMEM((n_col, PAD, local), F32),
                pltpu.VMEM((half_r + 1, PAD, local), F32),
                pltpu.VMEM((n_col, packed, 128), F32),
                pltpu.VMEM((half_r + 1, packed, 128), F32),
                pltpu.VMEM((n_col, packed, 128), F32),
                pltpu.VMEM((half_r + 1, packed, 128), F32),
                pltpu.VMEM((2, most, 8, 128), F32),
                pltpu.VMEM((2, 8, 128), F32),
                pltpu.VMEM((2, local, local), BF16),
                pltpu.VMEM((2, local, local), BF16),
                pltpu.SemaphoreType.DMA((3,)),
            ] + [pltpu.SemaphoreType.DMA((n,)) for n in counts for _ in range(2)],
            compiler_params=pltpu.CompilerParams(
                collective_id=0, has_side_effects=True, vmem_limit_bytes=48 << 20),
            name="subspace",
        )(points, spread, vectors)

    in_specs = (P(None, ("row", "col")), P(("row", "col")), P(None, ("row", "col")))
    return jax.shard_map(shards, mesh=mesh, in_specs=in_specs, out_specs=P(None, ("row", "col")), check_vma=False)
```

```python
import functools
import math

import jax
import jax.numpy as jnp
from jax import lax
from jax.experimental import pallas as pl
from jax.experimental.pallas import tpu as pltpu
from jax.sharding import PartitionSpec as P

F32, BF16 = jnp.float32, jnp.bfloat16
MESH = pl.DeviceIdType.MESH
LOG2E = 1.4426950408889634
DEPTH = 128
PAD = 16
PIECES_LEFT = (0, 0, 1, 1, 0, 2)
PIECES_RIGHT = (0, 1, 0, 1, 2, 0)


def split3(x):
    high = x.astype(BF16)
    rest = x - high.astype(F32)
    mid = rest.astype(BF16)
    low = (rest - mid.astype(F32)).astype(BF16)
    return high, mid, low


def factor(block, left):
    pts = block[:16].astype(F32)
    tail = block[16:].astype(F32)
    inv = 1.0 / tail[9:10]
    w = pts * inv
    norm = jnp.sum(pts * pts, axis=0, keepdims=True) * inv
    if left:
        w = w * (2.0 * LOG2E)
        terms = (norm * -LOG2E, inv * -LOG2E)
        order = PIECES_LEFT
    else:
        terms = (inv, norm)
        order = PIECES_RIGHT
    pieces = split3(w)
    rows = lax.broadcasted_iota(jnp.int32, pts.shape, 0)
    extra = jnp.zeros_like(pts)
    for t, term in enumerate(terms):
        cut = split3(term)
        for k, p in enumerate(order):
            extra = jnp.where(rows == 6 * t + k, cut[p].astype(F32), extra)
    return jnp.concatenate(
        [pieces[p] for p in order] + [extra.astype(BF16), jnp.zeros(pts.shape, BF16)], axis=0
    )


def kernel(n_row, n_col, pts_ref, spread_ref, vec_ref, out_ref, own, spread_v, vec_v, got_r, got_c, right, left,
           part_r, part_c, out_r, out_c, in_r, in_c, gram, gsend, aff, aff_t, load_sem, sems):
    half_r, half_c = n_row // 2, n_col // 2
    chunks = own.shape[1] // 128
    r, c = lax.axis_index("row"), lax.axis_index("col")
    local = own.shape[1]

    def at_row(d):
        return (lax.rem(r + d + n_row, n_row), c)

    def at_col(d):
        return (r, lax.rem(c + d + n_col, n_col))

    barrier = pltpu.get_barrier_semaphore()
    for d in range(1, n_col):
        pl.semaphore_signal(barrier, inc=1, device_id=at_col(d), device_id_type=MESH)
    for d in range(1, n_row):
        pl.semaphore_signal(barrier, inc=1, device_id=at_row(d), device_id_type=MESH)

    loads = [
        pltpu.make_async_copy(pts_ref, own.at[:16, :], load_sem.at[0]),
        pltpu.make_async_copy(vec_ref, vec_v, load_sem.at[1]),
        pltpu.make_async_copy(spread_ref, spread_v, load_sem.at[2]),
    ]
    for load in loads:
        load.start()
    part_r[...] = jnp.zeros_like(part_r)
    part_c[...] = jnp.zeros_like(part_c)
    gsend[...] = jnp.zeros_like(gsend)
    for load in loads:
        load.wait()
    rows8 = lax.broadcasted_iota(jnp.int32, (8, local), 0)
    spread = spread_v[...].astype(F32).reshape(1, local)
    tail = jnp.where(rows8 == 0, 1.0, jnp.where(rows8 == 1, spread, 0.0))
    own[16:, :] = jnp.concatenate([vec_v[...].astype(F32), tail], axis=0).astype(BF16)
    got_r[0] = own[...]
    got_c[0] = own[...]

    def copy(src, dst, name, slot, device):
        send, recv = sems[name]
        return pltpu.make_async_remote_copy(
            src_ref=src, dst_ref=dst.at[slot], send_sem=send.at[slot], recv_sem=recv.at[slot],
            device_id=device, device_id_type=MESH)

    def get_r(d):
        return copy(own, got_r, "gather_r", d, at_col(-d))

    def get_c(d):
        return copy(own, got_c, "gather_c", d, at_row(-d))

    def put_r(d):
        return copy(out_r.at[d], in_r, "reduce_r", d, at_col(d))

    def put_c(d):
        return copy(out_c.at[d], in_c, "reduce_c", d, at_row(d))

    def pack(dst, src):
        for n in range(chunks):
            lanes = pl.ds(128 * n, 128)
            dst[pl.ds(8 * n, 8), :] = src[:8, lanes]
            dst[pl.ds(8 * chunks + n, 1), :] = src[8:9, lanes]

    def add(totals, packed):
        product, degree = totals
        parts = [packed[pl.ds(8 * n, 8), :] for n in range(chunks)]
        degrees = packed[pl.ds(8 * chunks, chunks), :]
        return tuple(a + b for a, b in zip(product, parts)), degree + degrees

    def send_r(d):
        pack(out_r.at[d], part_r.at[d])
        put_r(d).start()

    def send_c(d):
        pack(out_c.at[d], part_c.at[d])
        put_c(d).start()

    def make_right(d):
        right[d] = factor(got_r[d], False)

    def make_left(d):
        left[d] = jnp.transpose(factor(got_c[d], True))

    def take_r(d):
        get_r(d).wait_recv()
        make_right(d)

    def take_c(d):
        get_c(d).wait_recv()
        make_left(d)

    half = local // 2

    def produce_part(slot, dr, dc, both, rows, lanes):
        expo = jnp.dot(left[dr, rows, :], right[dc, :, lanes], preferred_element_type=F32)
        affinity = jnp.exp2(expo).astype(BF16)
        aff[slot, rows, lanes] = affinity
        if both:
            aff_t[slot, lanes, rows] = jnp.transpose(affinity)

    def use_columns(slot, dr, dc, lanes):
        part_r[dc, :, lanes] += jnp.dot(got_c[dr, 16:, :], aff[slot, :, lanes], preferred_element_type=F32)

    def use_rows(slot, dr, dc, rows):
        part_c[dr, :, rows] += jnp.dot(got_r[dc, 16:, :], aff_t[slot, :, rows], preferred_element_type=F32)

    def step(cur, after):
        for q in range(4):
            rows, lanes = pl.ds((q // 2) * half, half), pl.ds((q % 2) * half, half)
            if cur is not None:
                slot, dr, dc, both = cur
                part = pl.ds((q % 2) * half, half)
                if q < 2:
                    use_columns(slot, dr, dc, part)
                elif both:
                    use_rows(slot, dr, dc, part)
            if after is not None:
                produce_part(*after, rows, lanes)

    make_right(0)
    make_left(0)
    step(None, (0, 0, 0, False))

    pl.semaphore_wait(barrier, n_row + n_col - 2)
    far_r = range(half_c + 1, n_col)
    square = min(4, half_r, half_c)
    for k in range(1, square):
        get_r(k).start()
        get_c(k).start()

    head = [(0, 0, False)]
    for k in range(1, square):
        for d in range(k):
            head += [(d, k, True), (k, d, True)]
        head.append((k, k, True))
    head += [(0, d, d < half_c) for d in range(square, half_c + 1)]
    first_row = len(head)
    head += [(dr, dc, True) for dr in range(1, square) for dc in range(square, half_c)]
    following = (square, 0, True) if square < half_r else (half_r, half_c, False)
    have_r, have_c = {0}, {0}
    for n, pair in enumerate(head):
        dr, dc, both = head[n + 1] if n + 1 < len(head) else following
        if n + 1 == first_row:
            for d in far_r:
                get_r(d).start()
            get_c(half_r).start()
        if dc not in have_r:
            if dc == min(2, square):
                for d in range(square, half_c + 1):
                    get_r(d).start()
            if dc == min(3, square):
                for d in range(square, half_r):
                    get_c(d).start()
            take_r(dc)
            have_r.add(dc)
        if dr not in have_c:
            take_c(dr)
            have_c.add(dr)
        step((n % 2, *pair), ((n + 1) % 2, dr, dc, both))
    done = len(head)

    def near(t, _):
        dr = square + t
        take_c(dr + 1)
        wrap = dr == half_r - 1
        for k in range(half_c):
            slot = (done + k) % 2
            after = (dr, k + 1) if k < half_c - 1 else (dr + 1, jnp.where(wrap, half_c, 0))
            step((slot, dr, k, True), (1 - slot, *after, True))
        return 0

    lax.fori_loop(0, half_r - square, near, 0)
    done += (half_r - square) * half_c

    for d in far_r:
        take_r(d)
    order = [half_c, 0] + list(range(1, half_c))
    for n, d in enumerate(order):
        slot = (done + n) % 2
        after = (half_r, order[n + 1], n >= 1) if n + 1 < len(order) else (1, half_c, True)
        step((slot, half_r, d, n >= 2), (1 - slot, *after))
    done += len(order)
    send_c(half_r)
    for d in range(1, half_c):
        send_r(d)

    def far(t, last):
        dc = half_c + 2 * t
        pairs = [(dc + e, dr) for e in range(2) for dr in range(1, half_r)]
        if not last:
            @pl.when(t > 0)
            def _():
                send_r(dc - 2)
                send_r(dc - 1)
        elif half_c > 2:
            send_r(dc - 2)
            send_r(dc - 1)
        for n, (d, dr) in enumerate(pairs):
            slot = (done + n) % 2
            after = None
            if n + 1 < len(pairs):
                after = (1 - slot, pairs[n + 1][1], pairs[n + 1][0], True)
            elif not last:
                after = (1 - slot, 1, dc + 2, True)
            step((slot, dr, d, True), after)
            if last and n == half_r - 2:
                send_r(d)
            if last and n >= half_r - 1:
                send_c(dr)
        if last:
            send_r(dc + 1)
        return 0

    lax.fori_loop(0, half_c // 2 - 1, lambda t, _: far(t, False), 0)
    far(half_c // 2 - 1, True)

    part_r[0] += part_c[0]
    pack(out_r.at[0], part_r.at[0])
    totals = (tuple(jnp.zeros((8, 128), F32) for _ in range(chunks)), jnp.zeros((chunks, 128), F32))
    totals = add(totals, out_r.at[0])
    put_c(half_r).wait_recv()
    totals = add(totals, in_c.at[half_r])
    for d in range(1, n_col - 1):
        put_r(d).wait_recv()
        totals = add(totals, in_r.at[d])
    for d in range(1, half_r):
        put_c(d).wait_recv()
        totals = add(totals, in_c.at[d])
    put_r(n_col - 1).wait_recv()
    product, degree = add(totals, in_r.at[n_col - 1])
    update = jnp.concatenate([product[n] / degree[n : n + 1] for n in range(chunks)], axis=1)
    mine = lax.dot_general(
        update, update, (((1,), (1,)), ((), ())), precision=lax.Precision.HIGHEST, preferred_element_type=F32)

    pending = []
    for stage, (count, place) in enumerate(((n_col, at_col), (n_row, at_row))):
        gsend[stage, :, :8] = mine
        puts = [copy(gsend.at[stage], gram.at[stage], ("gram_c", "gram_r")[stage], d, place(d)) for d in sorted(range(1, count), key=lambda d: -min(d % 8, 8 - d % 8))]
        for p in puts:
            p.start()
        acc = gsend[stage]
        for p in puts:
            p.wait_recv()
        for d in range(1, count):
            acc += gram[stage, d]
        mine = acc[:, :8]
        pending += puts

    g, u = mine, update
    rows_g = lax.broadcasted_iota(jnp.int32, g.shape, 0)
    rows_u = lax.broadcasted_iota(jnp.int32, u.shape, 0)
    for k in range(8):
        scale = lax.rsqrt(g[k : k + 1, k : k + 1])
        row_g, row_u = g[k : k + 1] * scale, u[k : k + 1] * scale
        col = g[:, k : k + 1] * scale
        u = jnp.where(rows_u == k, row_u, jnp.where(rows_u > k, u - col * row_u, u))
        g = jnp.where(rows_g > k, g - col * row_g, g)
    out_ref[...] = u * math.sqrt(local * n_row * n_col)

    for d in range(1, n_col):
        get_r(d).wait_send()
        put_r(d).wait_send()
    for d in range(1, half_r + 1):
        get_c(d).wait_send()
        put_c(d).wait_send()
    for p in pending:
        p.wait_send()


def run(n_row, n_col, *refs):
    refs, flat = refs[:-12], refs[-12:]
    names = ("gather_r", "gather_c", "reduce_r", "reduce_c", "gram_c", "gram_r")
    sems = {name: (flat[2 * i], flat[2 * i + 1]) for i, name in enumerate(names)}
    kernel(n_row, n_col, *refs, sems)


def solution(mesh):
    n_row, n_col = mesh.shape["row"], mesh.shape["col"]
    half_r = n_row // 2

    def shards(points, spread, vectors):
        local = points.shape[1]
        vmem = pl.BlockSpec(memory_space=pltpu.VMEM)
        counts = (n_col, half_r + 1, n_col, half_r + 1, n_col, n_row)
        most = max(n_row, n_col)
        packed = -(-9 * (local // 128) // 8) * 8
        return pl.pallas_call(
            functools.partial(run, n_row, n_col),
            out_shape=jax.ShapeDtypeStruct((8, local), F32),
            in_specs=[pl.BlockSpec(memory_space=pl.ANY)] * 3,
            out_specs=vmem,
            scratch_shapes=[
                pltpu.VMEM((32, local), BF16),
                pltpu.VMEM((local,), BF16),
                pltpu.VMEM((8, local), BF16),
                pltpu.VMEM((n_col, 32, local), BF16),
                pltpu.VMEM((half_r + 1, 32, local), BF16),
                pltpu.VMEM((n_col, DEPTH, local), BF16),
                pltpu.VMEM((half_r + 1, local, DEPTH), BF16),
                pltpu.VMEM((n_col, PAD, local), F32),
                pltpu.VMEM((half_r + 1, PAD, local), F32),
                pltpu.VMEM((n_col, packed, 128), F32),
                pltpu.VMEM((half_r + 1, packed, 128), F32),
                pltpu.VMEM((n_col, packed, 128), F32),
                pltpu.VMEM((half_r + 1, packed, 128), F32),
                pltpu.VMEM((2, most, 8, 128), F32),
                pltpu.VMEM((2, 8, 128), F32),
                pltpu.VMEM((2, local, local), BF16),
                pltpu.VMEM((2, local, local), BF16),
                pltpu.SemaphoreType.DMA((3,)),
            ] + [pltpu.SemaphoreType.DMA((n,)) for n in counts for _ in range(2)],
            compiler_params=pltpu.CompilerParams(
                collective_id=0, has_side_effects=True, vmem_limit_bytes=48 << 20),
            name="subspace",
        )(points, spread, vectors)

    in_specs = (P(None, ("row", "col")), P(("row", "col")), P(None, ("row", "col")))
    return jax.shard_map(shards, mesh=mesh, in_specs=in_specs, out_specs=P(None, ("row", "col")), check_vma=False)
```

```python
import functools
import math

import jax
import jax.numpy as jnp
from jax import lax
from jax.experimental import pallas as pl
from jax.experimental.pallas import tpu as pltpu
from jax.sharding import PartitionSpec as P

F32, BF16 = jnp.float32, jnp.bfloat16
MESH = pl.DeviceIdType.MESH
LOG2E = 1.4426950408889634
DEPTH = 128
PAD = 16
PIECES_LEFT = (0, 0, 1, 1, 0, 2)
PIECES_RIGHT = (0, 1, 0, 1, 2, 0)


def split3(x):
    high = x.astype(BF16)
    rest = x - high.astype(F32)
    mid = rest.astype(BF16)
    low = (rest - mid.astype(F32)).astype(BF16)
    return high, mid, low


def factor(block, left):
    pts = block[:16].astype(F32)
    tail = block[16:].astype(F32)
    inv = 1.0 / tail[9:10]
    w = pts * inv
    norm = jnp.sum(pts * pts, axis=0, keepdims=True) * inv
    if left:
        w = w * (2.0 * LOG2E)
        terms = (norm * -LOG2E, inv * -LOG2E)
        order = PIECES_LEFT
    else:
        terms = (inv, norm)
        order = PIECES_RIGHT
    pieces = split3(w)
    rows = lax.broadcasted_iota(jnp.int32, pts.shape, 0)
    extra = jnp.zeros_like(pts)
    for t, term in enumerate(terms):
        cut = split3(term)
        for k, p in enumerate(order):
            extra = jnp.where(rows == 6 * t + k, cut[p].astype(F32), extra)
    return jnp.concatenate(
        [pieces[p] for p in order] + [extra.astype(BF16), jnp.zeros(pts.shape, BF16)], axis=0
    )


def kernel(n_row, n_col, pts_ref, spread_ref, vec_ref, out_ref, own, spread_v, vec_v, got_r, got_c, right, left,
           part_r, part_c, out_r, out_c, in_r, in_c, gram, gsend, aff, aff_t, load_sem, sems):
    half_r, half_c = n_row // 2, n_col // 2
    chunks = own.shape[1] // 128
    r, c = lax.axis_index("row"), lax.axis_index("col")
    local = own.shape[1]

    def at_row(d):
        return (lax.rem(r + d + n_row, n_row), c)

    def at_col(d):
        return (r, lax.rem(c + d + n_col, n_col))

    barrier = pltpu.get_barrier_semaphore()
    for d in range(1, n_col):
        pl.semaphore_signal(barrier, inc=1, device_id=at_col(d), device_id_type=MESH)
    for d in range(1, n_row):
        pl.semaphore_signal(barrier, inc=1, device_id=at_row(d), device_id_type=MESH)

    loads = [
        pltpu.make_async_copy(pts_ref, own.at[:16, :], load_sem.at[0]),
        pltpu.make_async_copy(vec_ref, vec_v, load_sem.at[1]),
        pltpu.make_async_copy(spread_ref, spread_v, load_sem.at[2]),
    ]
    for load in loads:
        load.start()
    part_r[...] = jnp.zeros_like(part_r)
    part_c[...] = jnp.zeros_like(part_c)
    gsend[...] = jnp.zeros_like(gsend)
    for load in loads:
        load.wait()
    rows8 = lax.broadcasted_iota(jnp.int32, (8, local), 0)
    spread = spread_v[...].astype(F32).reshape(1, local)
    tail = jnp.where(rows8 == 0, 1.0, jnp.where(rows8 == 1, spread, 0.0))
    own[16:, :] = jnp.concatenate([vec_v[...].astype(F32), tail], axis=0).astype(BF16)
    got_r[0] = own[...]
    got_c[0] = own[...]

    def copy(src, dst, name, slot, device):
        send, recv = sems[name]
        return pltpu.make_async_remote_copy(
            src_ref=src, dst_ref=dst.at[slot], send_sem=send.at[slot], recv_sem=recv.at[slot],
            device_id=device, device_id_type=MESH)

    def get_r(d):
        return copy(own, got_r, "gather_r", d, at_col(-d))

    def get_c(d):
        return copy(own, got_c, "gather_c", d, at_row(-d))

    def put_r(d):
        return copy(out_r.at[d], in_r, "reduce_r", d, at_col(d))

    def put_c(d):
        return copy(out_c.at[d], in_c, "reduce_c", d, at_row(d))

    def pack(dst, src):
        for n in range(chunks):
            lanes = pl.ds(128 * n, 128)
            dst[pl.ds(8 * n, 8), :] = src[:8, lanes]
            dst[pl.ds(8 * chunks + n, 1), :] = src[8:9, lanes]

    def add(totals, packed):
        product, degree = totals
        parts = [packed[pl.ds(8 * n, 8), :] for n in range(chunks)]
        degrees = packed[pl.ds(8 * chunks, chunks), :]
        return tuple(a + b for a, b in zip(product, parts)), degree + degrees

    def send_r(d):
        pack(out_r.at[d], part_r.at[d])
        put_r(d).start()

    def send_c(d):
        pack(out_c.at[d], part_c.at[d])
        put_c(d).start()

    def make_right(d):
        right[d] = factor(got_r[d], False)

    def make_left(d):
        left[d] = jnp.transpose(factor(got_c[d], True))

    def take_r(d):
        get_r(d).wait_recv()
        make_right(d)

    def take_c(d):
        get_c(d).wait_recv()
        make_left(d)

    half = local // 2

    def produce_part(slot, dr, dc, both, rows, lanes):
        expo = jnp.dot(left[dr, rows, :], right[dc, :, lanes], preferred_element_type=F32)
        affinity = jnp.exp2(expo).astype(BF16)
        aff[slot, rows, lanes] = affinity
        if both:
            aff_t[slot, lanes, rows] = jnp.transpose(affinity)

    def use_columns(slot, dr, dc, lanes):
        part_r[dc, :, lanes] += jnp.dot(got_c[dr, 16:, :], aff[slot, :, lanes], preferred_element_type=F32)

    def use_rows(slot, dr, dc, rows):
        part_c[dr, :, rows] += jnp.dot(got_r[dc, 16:, :], aff_t[slot, :, rows], preferred_element_type=F32)

    def step(cur, after):
        for q in range(4):
            rows, lanes = pl.ds((q % 2) * half, half), pl.ds((q // 2) * half, half)
            if cur is not None:
                slot, dr, dc, both = cur
                part = pl.ds((q % 2) * half, half)
                if q < 2:
                    use_columns(slot, dr, dc, part)
                elif both:
                    use_rows(slot, dr, dc, part)
            if after is not None:
                produce_part(*after, rows, lanes)

    make_right(0)
    make_left(0)
    step(None, (0, 0, 0, False))

    pl.semaphore_wait(barrier, n_row + n_col - 2)
    far_r = range(half_c + 1, n_col)
    square = min(2, half_r, half_c)
    for k in range(1, square):
        get_r(k).start()
        get_c(k).start()
    for d in range(square, half_c + 1):
        get_r(d).start()

    head = [(0, 0, False)]
    for k in range(1, square):
        for d in range(k):
            head += [(d, k, True), (k, d, True)]
        head.append((k, k, True))
    head += [(0, d, d < half_c) for d in range(square, half_c + 1)]
    first_row = len(head)
    head += [(dr, dc, True) for dr in range(1, square) for dc in range(square, half_c)]
    following = (square, 0, True) if square < half_r else (half_r, half_c, False)
    have_r, have_c = {0}, {0}
    for n, pair in enumerate(head):
        dr, dc, both = head[n + 1] if n + 1 < len(head) else following
        if n + 1 == first_row:
            for d in far_r:
                get_r(d).start()
            get_c(half_r).start()
        if dc not in have_r:
            if dc == square:
                for d in range(square, half_r):
                    get_c(d).start()
            take_r(dc)
            have_r.add(dc)
        if dr not in have_c:
            take_c(dr)
            have_c.add(dr)
        step((n % 2, *pair), ((n + 1) % 2, dr, dc, both))
    done = len(head)

    def near(t, _):
        dr = square + t
        take_c(dr + 1)
        wrap = dr == half_r - 1
        for k in range(half_c):
            slot = (done + k) % 2
            after = (dr, k + 1) if k < half_c - 1 else (dr + 1, jnp.where(wrap, half_c, 0))
            step((slot, dr, k, True), (1 - slot, *after, True))
        return 0

    lax.fori_loop(0, half_r - square, near, 0)
    done += (half_r - square) * half_c

    for d in far_r:
        take_r(d)
    order = [half_c, 0] + list(range(1, half_c))
    for n, d in enumerate(order):
        slot = (done + n) % 2
        after = (half_r, order[n + 1], n >= 1) if n + 1 < len(order) else (1, half_c, True)
        step((slot, half_r, d, n >= 2), (1 - slot, *after))
    done += len(order)
    send_c(half_r)
    for d in range(1, half_c):
        send_r(d)

    def far(t, last):
        dc = half_c + 2 * t
        pairs = [(dc + e, dr) for e in range(2) for dr in range(1, half_r)]
        if not last:
            @pl.when(t > 0)
            def _():
                send_r(dc - 2)
                send_r(dc - 1)
        elif half_c > 2:
            send_r(dc - 2)
            send_r(dc - 1)
        for n, (d, dr) in enumerate(pairs):
            slot = (done + n) % 2
            after = None
            if n + 1 < len(pairs):
                after = (1 - slot, pairs[n + 1][1], pairs[n + 1][0], True)
            elif not last:
                after = (1 - slot, 1, dc + 2, True)
            step((slot, dr, d, True), after)
            if last and n == half_r - 2:
                send_r(d)
            if last and n >= half_r - 1:
                send_c(dr)
        if last:
            send_r(dc + 1)
        return 0

    lax.fori_loop(0, half_c // 2 - 1, lambda t, _: far(t, False), 0)
    far(half_c // 2 - 1, True)

    part_r[0] += part_c[0]
    pack(out_r.at[0], part_r.at[0])
    totals = (tuple(jnp.zeros((8, 128), F32) for _ in range(chunks)), jnp.zeros((chunks, 128), F32))
    totals = add(totals, out_r.at[0])
    put_c(half_r).wait_recv()
    totals = add(totals, in_c.at[half_r])
    for d in range(1, n_col - 1):
        put_r(d).wait_recv()
        totals = add(totals, in_r.at[d])
    for d in range(1, half_r):
        put_c(d).wait_recv()
        totals = add(totals, in_c.at[d])
    put_r(n_col - 1).wait_recv()
    product, degree = add(totals, in_r.at[n_col - 1])
    update = jnp.concatenate([product[n] / degree[n : n + 1] for n in range(chunks)], axis=1)
    mine = lax.dot_general(
        update, update, (((1,), (1,)), ((), ())), precision=lax.Precision.HIGHEST, preferred_element_type=F32)

    pending = []
    for stage, (count, place) in enumerate(((n_col, at_col), (n_row, at_row))):
        gsend[stage, :, :8] = mine
        puts = [copy(gsend.at[stage], gram.at[stage], ("gram_c", "gram_r")[stage], d, place(d)) for d in sorted(range(1, count), key=lambda d: -min(d % 8, 8 - d % 8))]
        for p in puts:
            p.start()
        acc = gsend[stage]
        for p in puts:
            p.wait_recv()
        for d in range(1, count):
            acc += gram[stage, d]
        mine = acc[:, :8]
        pending += puts

    g, u = mine, update
    rows_g = lax.broadcasted_iota(jnp.int32, g.shape, 0)
    rows_u = lax.broadcasted_iota(jnp.int32, u.shape, 0)
    for k in range(8):
        scale = lax.rsqrt(g[k : k + 1, k : k + 1])
        row_g, row_u = g[k : k + 1] * scale, u[k : k + 1] * scale
        col = g[:, k : k + 1] * scale
        u = jnp.where(rows_u == k, row_u, jnp.where(rows_u > k, u - col * row_u, u))
        g = jnp.where(rows_g > k, g - col * row_g, g)
    out_ref[...] = u * math.sqrt(local * n_row * n_col)

    for d in range(1, n_col):
        get_r(d).wait_send()
        put_r(d).wait_send()
    for d in range(1, half_r + 1):
        get_c(d).wait_send()
        put_c(d).wait_send()
    for p in pending:
        p.wait_send()


def run(n_row, n_col, *refs):
    refs, flat = refs[:-12], refs[-12:]
    names = ("gather_r", "gather_c", "reduce_r", "reduce_c", "gram_c", "gram_r")
    sems = {name: (flat[2 * i], flat[2 * i + 1]) for i, name in enumerate(names)}
    kernel(n_row, n_col, *refs, sems)


def solution(mesh):
    n_row, n_col = mesh.shape["row"], mesh.shape["col"]
    half_r = n_row // 2

    def shards(points, spread, vectors):
        local = points.shape[1]
        vmem = pl.BlockSpec(memory_space=pltpu.VMEM)
        counts = (n_col, half_r + 1, n_col, half_r + 1, n_col, n_row)
        most = max(n_row, n_col)
        packed = -(-9 * (local // 128) // 8) * 8
        return pl.pallas_call(
            functools.partial(run, n_row, n_col),
            out_shape=jax.ShapeDtypeStruct((8, local), F32),
            in_specs=[pl.BlockSpec(memory_space=pl.ANY)] * 3,
            out_specs=vmem,
            scratch_shapes=[
                pltpu.VMEM((32, local), BF16),
                pltpu.VMEM((local,), BF16),
                pltpu.VMEM((8, local), BF16),
                pltpu.VMEM((n_col, 32, local), BF16),
                pltpu.VMEM((half_r + 1, 32, local), BF16),
                pltpu.VMEM((n_col, DEPTH, local), BF16),
                pltpu.VMEM((half_r + 1, local, DEPTH), BF16),
                pltpu.VMEM((n_col, PAD, local), F32),
                pltpu.VMEM((half_r + 1, PAD, local), F32),
                pltpu.VMEM((n_col, packed, 128), F32),
                pltpu.VMEM((half_r + 1, packed, 128), F32),
                pltpu.VMEM((n_col, packed, 128), F32),
                pltpu.VMEM((half_r + 1, packed, 128), F32),
                pltpu.VMEM((2, most, 8, 128), F32),
                pltpu.VMEM((2, 8, 128), F32),
                pltpu.VMEM((2, local, local), BF16),
                pltpu.VMEM((2, local, local), BF16),
                pltpu.SemaphoreType.DMA((3,)),
            ] + [pltpu.SemaphoreType.DMA((n,)) for n in counts for _ in range(2)],
            compiler_params=pltpu.CompilerParams(
                collective_id=0, has_side_effects=True, vmem_limit_bytes=48 << 20),
            name="subspace",
        )(points, spread, vectors)

    in_specs = (P(None, ("row", "col")), P(("row", "col")), P(None, ("row", "col")))
    return jax.shard_map(shards, mesh=mesh, in_specs=in_specs, out_specs=P(None, ("row", "col")), check_vma=False)
```

```python
import functools
import math

import jax
import jax.numpy as jnp
from jax import lax
from jax.experimental import pallas as pl
from jax.experimental.pallas import tpu as pltpu
from jax.sharding import PartitionSpec as P

F32, BF16 = jnp.float32, jnp.bfloat16
MESH = pl.DeviceIdType.MESH
LOG2E = 1.4426950408889634
DEPTH = 128
PAD = 16
PIECES_LEFT = (0, 0, 1, 1, 0, 2)
PIECES_RIGHT = (0, 1, 0, 1, 2, 0)


def split3(x):
    high = x.astype(BF16)
    rest = x - high.astype(F32)
    mid = rest.astype(BF16)
    low = (rest - mid.astype(F32)).astype(BF16)
    return high, mid, low


def factor(block, left):
    pts = block[:16].astype(F32)
    tail = block[16:].astype(F32)
    inv = 1.0 / tail[9:10]
    w = pts * inv
    norm = jnp.sum(pts * pts, axis=0, keepdims=True) * inv
    if left:
        w = w * (2.0 * LOG2E)
        terms = (norm * -LOG2E, inv * -LOG2E)
        order = PIECES_LEFT
    else:
        terms = (inv, norm)
        order = PIECES_RIGHT
    pieces = split3(w)
    rows = lax.broadcasted_iota(jnp.int32, pts.shape, 0)
    extra = jnp.zeros_like(pts)
    for t, term in enumerate(terms):
        cut = split3(term)
        for k, p in enumerate(order):
            extra = jnp.where(rows == 6 * t + k, cut[p].astype(F32), extra)
    return jnp.concatenate(
        [pieces[p] for p in order] + [extra.astype(BF16), jnp.zeros(pts.shape, BF16)], axis=0
    )


def kernel(n_row, n_col, pts_ref, spread_ref, vec_ref, out_ref, own, spread_v, vec_v, got_r, got_c, right, left,
           part_r, part_c, out_r, out_c, in_r, in_c, gram, gsend, aff, aff_t, load_sem, sems):
    half_r, half_c = n_row // 2, n_col // 2
    chunks = own.shape[1] // 128
    r, c = lax.axis_index("row"), lax.axis_index("col")
    local = own.shape[1]

    def at_row(d):
        return (lax.rem(r + d + n_row, n_row), c)

    def at_col(d):
        return (r, lax.rem(c + d + n_col, n_col))

    barrier = pltpu.get_barrier_semaphore()
    for d in range(1, n_col):
        pl.semaphore_signal(barrier, inc=1, device_id=at_col(d), device_id_type=MESH)
    for d in range(1, n_row):
        pl.semaphore_signal(barrier, inc=1, device_id=at_row(d), device_id_type=MESH)

    loads = [
        pltpu.make_async_copy(pts_ref, own.at[:16, :], load_sem.at[0]),
        pltpu.make_async_copy(vec_ref, vec_v, load_sem.at[1]),
        pltpu.make_async_copy(spread_ref, spread_v, load_sem.at[2]),
    ]
    for load in loads:
        load.start()
    part_r[...] = jnp.zeros_like(part_r)
    part_c[...] = jnp.zeros_like(part_c)
    gsend[...] = jnp.zeros_like(gsend)
    for load in loads:
        load.wait()
    rows8 = lax.broadcasted_iota(jnp.int32, (8, local), 0)
    spread = spread_v[...].astype(F32).reshape(1, local)
    tail = jnp.where(rows8 == 0, 1.0, jnp.where(rows8 == 1, spread, 0.0))
    own[16:, :] = jnp.concatenate([vec_v[...].astype(F32), tail], axis=0).astype(BF16)
    got_r[0] = own[...]
    got_c[0] = own[...]

    def copy(src, dst, name, slot, device):
        send, recv = sems[name]
        return pltpu.make_async_remote_copy(
            src_ref=src, dst_ref=dst.at[slot], send_sem=send.at[slot], recv_sem=recv.at[slot],
            device_id=device, device_id_type=MESH)

    def get_r(d):
        return copy(own, got_r, "gather_r", d, at_col(-d))

    def get_c(d):
        return copy(own, got_c, "gather_c", d, at_row(-d))

    def put_r(d):
        return copy(out_r.at[d], in_r, "reduce_r", d, at_col(d))

    def put_c(d):
        return copy(out_c.at[d], in_c, "reduce_c", d, at_row(d))

    def pack(dst, src):
        for n in range(chunks):
            lanes = pl.ds(128 * n, 128)
            dst[pl.ds(8 * n, 8), :] = src[:8, lanes]
            dst[pl.ds(8 * chunks + n, 1), :] = src[8:9, lanes]

    def add(totals, packed):
        product, degree = totals
        parts = [packed[pl.ds(8 * n, 8), :] for n in range(chunks)]
        degrees = packed[pl.ds(8 * chunks, chunks), :]
        return tuple(a + b for a, b in zip(product, parts)), degree + degrees

    def send_r(d):
        pack(out_r.at[d], part_r.at[d])
        put_r(d).start()

    def send_c(d):
        pack(out_c.at[d], part_c.at[d])
        put_c(d).start()

    def make_right(d):
        right[d] = factor(got_r[d], False)

    def make_left(d):
        left[d] = jnp.transpose(factor(got_c[d], True))

    def take_r(d):
        get_r(d).wait_recv()
        make_right(d)

    def take_c(d):
        get_c(d).wait_recv()
        make_left(d)

    half = local // 2

    def produce_part(slot, dr, dc, both, rows, lanes):
        expo = jnp.dot(left[dr, rows, :], right[dc, :, lanes], preferred_element_type=F32)
        affinity = jnp.exp2(expo).astype(BF16)
        aff[slot, rows, lanes] = affinity
        if both:
            aff_t[slot, lanes, rows] = jnp.transpose(affinity)

    def use_columns(slot, dr, dc, lanes):
        part_r[dc, :, lanes] += jnp.dot(got_c[dr, 16:, :], aff[slot, :, lanes], preferred_element_type=F32)

    def use_rows(slot, dr, dc, rows):
        part_c[dr, :, rows] += jnp.dot(got_r[dc, 16:, :], aff_t[slot, :, rows], preferred_element_type=F32)

    def step(cur, after):
        for q in range(4):
            rows, lanes = pl.ds((q % 2) * half, half), pl.ds((q // 2) * half, half)
            if cur is not None:
                slot, dr, dc, both = cur
                part = pl.ds((q % 2) * half, half)
                if q < 2:
                    use_columns(slot, dr, dc, part)
                elif both:
                    use_rows(slot, dr, dc, part)
            if after is not None:
                produce_part(*after, rows, lanes)

    make_right(0)
    make_left(0)
    step(None, (0, 0, 0, False))

    pl.semaphore_wait(barrier, n_row + n_col - 2)
    far_r = range(half_c + 1, n_col)
    square = min(2, half_r, half_c)
    for k in range(1, square):
        get_r(k).start()
        get_c(k).start()
    nearest = sorted(range(square, half_c + 1), key=lambda d: min(d % half_c, half_c - d % half_c))
    for d in nearest:
        get_r(d).start()

    head = [(0, 0, False)]
    for k in range(1, square):
        for d in range(k):
            head += [(d, k, True), (k, d, True)]
        head.append((k, k, True))
    for d in nearest:
        head.append((0, d, d < half_c))
        if d < half_c:
            head += [(dr, d, True) for dr in range(1, square)]
    following = (square, 0, True) if square < half_r else (half_r, half_c, False)
    have_r, have_c = {0}, {0}
    for n, pair in enumerate(head):
        dr, dc, both = head[n + 1] if n + 1 < len(head) else following
        if n + 2 == len(head):
            for d in far_r:
                get_r(d).start()
            get_c(half_r).start()
        if dc not in have_r:
            if dc == nearest[0]:
                for d in range(square, half_r):
                    get_c(d).start()
            take_r(dc)
            have_r.add(dc)
        if dr not in have_c:
            take_c(dr)
            have_c.add(dr)
        step((n % 2, *pair), ((n + 1) % 2, dr, dc, both))
    done = len(head)

    def near(t, _):
        dr = square + t
        take_c(dr + 1)
        wrap = dr == half_r - 1
        for k in range(half_c):
            slot = (done + k) % 2
            after = (dr, k + 1) if k < half_c - 1 else (dr + 1, jnp.where(wrap, half_c, 0))
            step((slot, dr, k, True), (1 - slot, *after, True))
        return 0

    lax.fori_loop(0, half_r - square, near, 0)
    done += (half_r - square) * half_c

    for d in far_r:
        take_r(d)
    order = [half_c, 0] + list(range(1, half_c))
    for n, d in enumerate(order):
        slot = (done + n) % 2
        after = (half_r, order[n + 1], n >= 1) if n + 1 < len(order) else (1, half_c, True)
        step((slot, half_r, d, n >= 2), (1 - slot, *after))
    done += len(order)
    send_c(half_r)
    for d in range(1, half_c):
        send_r(d)

    def far(t, last):
        dc = half_c + 2 * t
        pairs = [(dc + e, dr) for e in range(2) for dr in range(1, half_r)]
        if not last:
            @pl.when(t > 0)
            def _():
                send_r(dc - 2)
                send_r(dc - 1)
        elif half_c > 2:
            send_r(dc - 2)
            send_r(dc - 1)
        for n, (d, dr) in enumerate(pairs):
            slot = (done + n) % 2
            after = None
            if n + 1 < len(pairs):
                after = (1 - slot, pairs[n + 1][1], pairs[n + 1][0], True)
            elif not last:
                after = (1 - slot, 1, dc + 2, True)
            step((slot, dr, d, True), after)
            if last and n == half_r - 2:
                send_r(d)
            if last and n >= half_r - 1:
                send_c(dr)
        if last:
            send_r(dc + 1)
        return 0

    lax.fori_loop(0, half_c // 2 - 1, lambda t, _: far(t, False), 0)
    far(half_c // 2 - 1, True)

    part_r[0] += part_c[0]
    pack(out_r.at[0], part_r.at[0])
    totals = (tuple(jnp.zeros((8, 128), F32) for _ in range(chunks)), jnp.zeros((chunks, 128), F32))
    totals = add(totals, out_r.at[0])
    put_c(half_r).wait_recv()
    totals = add(totals, in_c.at[half_r])
    for d in range(1, n_col - 1):
        put_r(d).wait_recv()
        totals = add(totals, in_r.at[d])
    for d in range(1, half_r):
        put_c(d).wait_recv()
        totals = add(totals, in_c.at[d])
    put_r(n_col - 1).wait_recv()
    product, degree = add(totals, in_r.at[n_col - 1])
    update = jnp.concatenate([product[n] / degree[n : n + 1] for n in range(chunks)], axis=1)
    mine = lax.dot_general(
        update, update, (((1,), (1,)), ((), ())), precision=lax.Precision.HIGHEST, preferred_element_type=F32)

    pending = []
    for stage, (count, place) in enumerate(((n_col, at_col), (n_row, at_row))):
        gsend[stage, :, :8] = mine
        puts = [copy(gsend.at[stage], gram.at[stage], ("gram_c", "gram_r")[stage], d, place(d)) for d in sorted(range(1, count), key=lambda d: -min(d % 8, 8 - d % 8))]
        for p in puts:
            p.start()
        acc = gsend[stage]
        for p in puts:
            p.wait_recv()
        for d in range(1, count):
            acc += gram[stage, d]
        mine = acc[:, :8]
        pending += puts

    g, u = mine, update
    rows_g = lax.broadcasted_iota(jnp.int32, g.shape, 0)
    rows_u = lax.broadcasted_iota(jnp.int32, u.shape, 0)
    for k in range(8):
        scale = lax.rsqrt(g[k : k + 1, k : k + 1])
        row_g, row_u = g[k : k + 1] * scale, u[k : k + 1] * scale
        col = g[:, k : k + 1] * scale
        u = jnp.where(rows_u == k, row_u, jnp.where(rows_u > k, u - col * row_u, u))
        g = jnp.where(rows_g > k, g - col * row_g, g)
    out_ref[...] = u * math.sqrt(local * n_row * n_col)

    for d in range(1, n_col):
        get_r(d).wait_send()
        put_r(d).wait_send()
    for d in range(1, half_r + 1):
        get_c(d).wait_send()
        put_c(d).wait_send()
    for p in pending:
        p.wait_send()


def run(n_row, n_col, *refs):
    refs, flat = refs[:-12], refs[-12:]
    names = ("gather_r", "gather_c", "reduce_r", "reduce_c", "gram_c", "gram_r")
    sems = {name: (flat[2 * i], flat[2 * i + 1]) for i, name in enumerate(names)}
    kernel(n_row, n_col, *refs, sems)


def solution(mesh):
    n_row, n_col = mesh.shape["row"], mesh.shape["col"]
    half_r = n_row // 2

    def shards(points, spread, vectors):
        local = points.shape[1]
        vmem = pl.BlockSpec(memory_space=pltpu.VMEM)
        counts = (n_col, half_r + 1, n_col, half_r + 1, n_col, n_row)
        most = max(n_row, n_col)
        packed = -(-9 * (local // 128) // 8) * 8
        return pl.pallas_call(
            functools.partial(run, n_row, n_col),
            out_shape=jax.ShapeDtypeStruct((8, local), F32),
            in_specs=[pl.BlockSpec(memory_space=pl.ANY)] * 3,
            out_specs=vmem,
            scratch_shapes=[
                pltpu.VMEM((32, local), BF16),
                pltpu.VMEM((local,), BF16),
                pltpu.VMEM((8, local), BF16),
                pltpu.VMEM((n_col, 32, local), BF16),
                pltpu.VMEM((half_r + 1, 32, local), BF16),
                pltpu.VMEM((n_col, DEPTH, local), BF16),
                pltpu.VMEM((half_r + 1, local, DEPTH), BF16),
                pltpu.VMEM((n_col, PAD, local), F32),
                pltpu.VMEM((half_r + 1, PAD, local), F32),
                pltpu.VMEM((n_col, packed, 128), F32),
                pltpu.VMEM((half_r + 1, packed, 128), F32),
                pltpu.VMEM((n_col, packed, 128), F32),
                pltpu.VMEM((half_r + 1, packed, 128), F32),
                pltpu.VMEM((2, most, 8, 128), F32),
                pltpu.VMEM((2, 8, 128), F32),
                pltpu.VMEM((2, local, local), BF16),
                pltpu.VMEM((2, local, local), BF16),
                pltpu.SemaphoreType.DMA((3,)),
            ] + [pltpu.SemaphoreType.DMA((n,)) for n in counts for _ in range(2)],
            compiler_params=pltpu.CompilerParams(
                collective_id=0, has_side_effects=True, vmem_limit_bytes=48 << 20),
            name="subspace",
        )(points, spread, vectors)

    in_specs = (P(None, ("row", "col")), P(("row", "col")), P(None, ("row", "col")))
    return jax.shard_map(shards, mesh=mesh, in_specs=in_specs, out_specs=P(None, ("row", "col")), check_vma=False)
```
